32 devices in a mesh: grp: 2 (over x), scan: 8 (over z, y), det: 2 (over core).
Axes of the slice: x: 2, y: 2, z: 4, core: 2. Of those that a mesh axis runs over, the one named last changes fastest.
Arguments:
- spectra: float32 [16384, 4096], P(('grp', 'scan'), 'det'), parts along dimension 0, may hold values from 0 to 544, as said below
- basis: float32 [64, 4096], P('grp', 'det'), parts along dimension 0, may hold values from 0.03 to 8, as said below
- loadings: float32 [64, 8192], P('grp', 'scan'), parts along dimension 0, may hold values from 0.005 to 6, as said below
Outputs:
- new_loadings: float32 [64, 8192], P('grp', 'scan'), parts along dimension 0
- new_basis: float32 [64, 4096], P('grp', 'det'), parts along dimension 0
The draws below stay inside these ranges and needn't reach their ends.
There are 2 independent parts, one for each index of `grp`. The reference program is written for one: setup_inputs(seed, part) draws one part's arguments, and reference() takes and returns one part's arrays. A program takes and returns all parts, laid end to end along the dimension named above; each array names one. Nothing has to cross between parts.
Inputs may be any that keep to these rules, and one draw needn't show every extreme that they name: `spectra`: intensities are nonnegative. `basis`: entries are positive. `loadings`: entries are positive.
All inputs are finite; a program needn't handle non-finite values.
Results may differ from the reference program's by a relative error of at most 0.00005.
Values sent between devices are 32-bit elements; how exact they have to be, the bound alone decides.
A program may use at most 64 MiB of HBM per device.

```python
import math
import jax
import jax.numpy as jnp
from jax import lax

Q = 4096
R = 32
POSITIONS = 8192


def truth(key):
    side = math.isqrt(Q)
    cell = jnp.arange(Q, dtype=jnp.int32)
    row_pos = (cell // side).astype(jnp.float32)
    col_pos = (cell % side).astype(jnp.float32)
    key_center = jax.random.fold_in(key, 101)
    key_radius = jax.random.fold_in(key, 102)
    key_amp = jax.random.fold_in(key, 103)
    key_gain = jax.random.fold_in(key, 104)
    key_block = jax.random.fold_in(key, 105)
    key_entry = jax.random.fold_in(key, 106)
    centers = jax.random.uniform(key_center, (R, 2), jnp.float32, 0.0, side - 1.0)
    radius = side * jax.random.uniform(key_radius, (R, 1), jnp.float32, 0.06, 0.2)
    amplitude = jax.random.uniform(key_amp, (R, 1), jnp.float32, 1.0, 2.0)
    gain = jax.random.uniform(key_gain, (Q,), jnp.float32, 0.5, 1.5)
    background = 0.15
    row_off = row_pos[None, :] - centers[:, 0:1]
    col_off = col_pos[None, :] - centers[:, 1:2]
    dist = row_off * row_off + col_off * col_off
    pattern = (background + amplitude * jnp.exp(-dist / (2.0 * radius * radius))) * gain[None, :]
    block_count = POSITIONS // 16
    block_scale = jnp.exp(jax.random.uniform(key_block, (R, block_count), jnp.float32, math.log(0.02), math.log(2.0)))
    entry = jax.random.uniform(key_entry, (R, POSITIONS), jnp.float32, 0.5, 1.5)
    abundance = jnp.repeat(block_scale, 16, axis=1) * entry
    return (pattern, abundance)


def draw_spectra(key, part):
    pattern, abundance = truth(key)
    clean = jnp.dot(abundance.T, pattern, precision=lax.Precision.HIGHEST)
    key_noise = jax.random.fold_in(key, 201)
    key_offset = jax.random.fold_in(key, 202)
    factor = jax.random.uniform(key_noise, (POSITIONS, Q), jnp.float32, 0.6, 1.4)
    offset = jax.random.uniform(key_offset, (POSITIONS, Q), jnp.float32, 0.0, 0.5)
    return clean * factor + offset


def draw_basis(key, part):
    pattern, abundance = truth(key)
    key_noise = jax.random.fold_in(key, 301)
    factor = jnp.exp(jax.random.uniform(key_noise, (R, Q), jnp.float32, math.log(0.5), math.log(2.0)))
    return pattern * factor


def draw_loadings(key, part):
    pattern, abundance = truth(key)
    key_noise = jax.random.fold_in(key, 401)
    factor = jnp.exp(jax.random.uniform(key_noise, (R, POSITIONS), jnp.float32, math.log(0.5), math.log(2.0)))
    return abundance * factor


def setup_inputs(seed: int = 0, part: int = 0) -> dict:
    splits = jax.random.split(jax.random.key(seed), 4)
    part_splits = jax.random.split(jax.random.fold_in(splits[3], part), 4)
    spectra = draw_spectra(jax.random.fold_in(jax.random.fold_in(splits[3], part), 71), part)
    basis = draw_basis(jax.random.fold_in(jax.random.fold_in(splits[3], part), 71), part)
    loadings = draw_loadings(jax.random.fold_in(jax.random.fold_in(splits[3], part), 71), part)
    return dict(spectra=spectra, basis=basis, loadings=loadings)


HIGHEST = lax.Precision.HIGHEST


def reference(spectra, basis, loadings):
    tied = 0.5 * (basis + jnp.flip(basis, 1))
    numer_h = lax.dot_general(tied, spectra, (((1,), (1,)), ((), ())), precision=HIGHEST)
    gram = lax.dot_general(tied, tied, (((1,), (1,)), ((), ())), precision=HIGHEST)
    new_loadings = loadings * numer_h / jnp.dot(gram, loadings, precision=HIGHEST)
    numer_w = jnp.dot(new_loadings, spectra, precision=HIGHEST)
    cross = lax.dot_general(new_loadings, new_loadings, (((1,), (1,)), ((), ())), precision=HIGHEST)
    tied_numer = 0.5 * (numer_w + jnp.flip(numer_w, 1))
    new_basis = tied * tied_numer / jnp.dot(cross, tied, precision=HIGHEST)
    return new_loadings, new_basis
```

```python
import functools

import jax
import jax.numpy as jnp
from jax import lax
from jax.experimental import pallas as pl
from jax.experimental.pallas import tpu as pltpu
from jax.sharding import PartitionSpec as P

HIGHEST = lax.Precision.HIGHEST
MESH = pl.DeviceIdType.MESH
F32 = jnp.float32
BF16 = jnp.bfloat16
LANES = 128


def split(x):
    hi = x.astype(BF16)
    lo = (x - hi.astype(F32)).astype(BF16)
    return hi, lo


def dot_nt(a, b):
    return lax.dot_general(a, b, (((1,), (1,)), ((), ())), preferred_element_type=F32)


def dot_nn(a, b):
    return lax.dot_general(a, b, (((1,), (0,)), ((), ())), preferred_element_type=F32)


def mirrored(x):
    index = (LANES - 1) - lax.broadcasted_iota(jnp.int32, x.shape, 1)
    return jnp.take_along_axis(x, index, axis=1, mode="promise_in_bounds")


def kernel(
    n, load_chunks, pos_chunk, col_chunk, barrier_at,
    spectra, basis, loadings, new_loadings, new_basis,
    sbuf, s_hi, s_lo, own, other, load, tied3, tied2, num_out, num_in, nl2,
    w_keep, w_out, w_in, rs_in, cr_out, cr_in, piece_buf, ag_in, fw_in,
    sp_sem, io_sem, bs_sem, nm_sem, w_sem, rs_send, rs_recv, cr_send, cr_recv,
    ag_send, ag_recv, fw_send, fw_recv,
):
    rank, pixels = basis.shape
    positions = loadings.shape[1]
    blocks = pixels // LANES
    half = blocks // 2
    if n <= half:
        per, row_split = half // n, 1
    else:
        per, row_split = 1, min(n // half, rank // 8)
    owners = half // per * row_split
    rows = rank // row_split
    pack = LANES // rank
    me = lax.axis_index("scan")
    det = lax.axis_index("det")
    partner = {"det": 1 - det}

    def peer(k):
        return lax.rem(me + k, n)

    def source(k):
        return lax.rem(me + n - k, n)

    def owner_only(index, fn):
        if owners == n:
            fn()
        else:
            pl.when(index < owners)(fn)

    def piece_at(index):
        first = index // row_split * per
        row = pl.multiple_of(lax.rem(index, row_split) * rows, 8) if row_split > 1 else 0
        return pl.ds(first, per), pl.ds(row, rows)

    def remote(src, dst, send, recv, where):
        return pltpu.make_async_remote_copy(
            src_ref=src, dst_ref=dst, send_sem=send, recv_sem=recv,
            device_id=where, device_id_type=MESH,
        )

    barrier = pltpu.get_barrier_semaphore()
    pl.semaphore_signal(barrier, inc=1, device_id=partner, device_id_type=MESH)
    for k in range(1, n):
        pl.semaphore_signal(barrier, inc=1, device_id={"scan": peer(k)}, device_id_type=MESH)

    own_copy = pltpu.make_async_copy(basis, own, io_sem.at[0])
    own_copy.start()
    load_rows = positions // load_chunks
    spectra_copies = []
    for i in range(load_chunks):
        part = pl.ds(i * load_rows, load_rows)
        spectra_copies.append(
            pltpu.make_async_copy(spectra.at[part], sbuf.at[part], sp_sem.at[i])
        )
        spectra_copies[i].start()
    load_copy = pltpu.make_async_copy(loadings, load, io_sem.at[1])
    load_copy.start()

    basis_copy = remote(own, other, bs_sem.at[0], bs_sem.at[1], partner)

    def enter():
        own_copy.wait()
        pl.semaphore_wait(barrier, n)
        basis_copy.start()

    for i in range(load_chunks):
        if i == barrier_at:
            enter()
        spectra_copies[i].wait()

        @pl.loop(0, load_rows // 16)
        def _(j):
            part = pl.ds(pl.multiple_of(i * load_rows + j * 16, 16), 16)
            hi, lo = split(sbuf[part, :])
            s_hi[part, :] = hi
            s_lo[part, :] = lo

    if barrier_at >= load_chunks:
        enter()

    basis_copy.wait()
    for b in range(blocks):
        mine = own[:, b * LANES:(b + 1) * LANES]
        back = blocks - 1 - b
        tied = 0.5 * (mine + mirrored(other[:, back * LANES:(back + 1) * LANES]))
        tied3[b] = tied
        hi, lo = split(tied)
        tied2[:rank, b * LANES:(b + 1) * LANES] = hi
        tied2[rank:, b * LANES:(b + 1) * LANES] = lo

    num_copies = []
    for i in range(positions // pos_chunk):
        part = pl.ds(i * pos_chunk, pos_chunk)
        both = dot_nt(tied2[...], s_hi[part, :])
        low = dot_nt(tied2[:rank, :], s_lo[part, :])
        num_out[i] = both[:rank] + (both[rank:] + low)
        num_copies.append(
            remote(num_out.at[i], num_in.at[i], nm_sem.at[0, i], nm_sem.at[1, i], partner)
        )
        num_copies[i].start()

    squares = dot_nt(tied2[...], tied2[...])
    gram = 2.0 * (
        squares[:rank, :rank] + (squares[:rank, rank:] + squares[rank:, :rank])
    )
    load_copy.wait()
    weighted = jnp.dot(gram, load[...], precision=HIGHEST, preferred_element_type=F32)

    for i in range(positions // pos_chunk):
        num_copies[i].wait()
        cols = slice(i * pos_chunk, (i + 1) * pos_chunk)
        fresh = load[:, cols] * (num_out[i] + num_in[i]) / weighted[:, cols]
        new_loadings[:, cols] = fresh
        hi, lo = split(fresh)
        nl2[:rank, cols] = hi
        nl2[rank:, cols] = lo

    squares = dot_nt(nl2[...], nl2[...])
    cross = squares[:rank, :rank] + (squares[:rank, rank:] + squares[rank:, :rank])
    cr_out[...] = jnp.concatenate(
        [cross[i * (rank // pack):(i + 1) * (rank // pack)] for i in range(pack)], axis=1
    )
    cr_copies = [None]
    for k in range(1, n):
        cr_copies.append(
            remote(cr_out, cr_in.at[k], cr_send.at[k], cr_recv.at[k], {"scan": peer(k)})
        )
        cr_copies[k].start()

    def sums(cols):
        both = dot_nn(nl2[...], s_hi[:, cols])
        low = dot_nn(nl2[:rank, :], s_lo[:, cols])
        return both[:rank] + (both[rank:] + low)

    step = col_chunk // LANES
    w_copies = []
    for i in range(half // step):
        first = half + i * step
        value = sums(slice(first * LANES, (first + step) * LANES))
        for j in range(step):
            w_out[i * step + j] = value[:, j * LANES:(j + 1) * LANES]
        part = pl.ds(i * step, step)
        w_copies.append(
            remote(w_out.at[part], w_in.at[part], w_sem.at[0, i], w_sem.at[1, i], partner)
        )
        w_copies[i].start()
    for i in range(half // step):
        value = sums(slice(i * col_chunk, (i + 1) * col_chunk))
        for j in range(step):
            w_keep[i * step + j] = value[:, j * LANES:(j + 1) * LANES]
    for copy in w_copies:
        copy.wait()
    for b in range(half):
        w_keep[b] = w_keep[b] + mirrored(w_in[half - 1 - b])

    rs_copies = [None]
    for k in range(1, n):
        rs_copies.append(
            remote(
                w_keep.at[piece_at(peer(k))], rs_in.at[k], rs_send.at[k], rs_recv.at[k],
                {"scan": peer(k)},
            )
        )
        owner_only(peer(k), rs_copies[k].start)

    for k in range(1, n):
        cr_copies[k].wait()
    packed = cr_out[...]
    for k in range(1, n):
        packed = packed + cr_in[k]
    cross = jnp.concatenate(
        [packed[:, i * rank:(i + 1) * rank] for i in range(pack)], axis=0
    )

    ag_copies = [None]
    for k in range(1, n):
        ag_copies.append(
            remote(piece_buf, ag_in.at[k], ag_send.at[k], ag_recv.at[k], {"scan": peer(k)})
        )
    fw_copies = [remote(piece_buf, fw_in.at[0], fw_send.at[0], fw_recv.at[0], partner)]
    for k in range(1, n):
        fw_copies.append(
            remote(ag_in.at[k], fw_in.at[k], fw_send.at[k], fw_recv.at[k], partner)
        )

    def own_piece():
        first, row = piece_at(me)
        for j in range(per):
            weights = jnp.dot(
                cross, tied3[first.start + j], precision=HIGHEST, preferred_element_type=F32
            )
            if row_split > 1:
                piece_buf[0] = weights[:rows]
                for i in range(1, row_split):
                    @pl.when(lax.rem(me, row_split) == i)
                    def _():
                        piece_buf[0] = weights[i * rows:(i + 1) * rows]
            else:
                piece_buf[j] = weights
        for k in range(1, n):
            rs_copies[k].wait_recv()
        for j in range(per):
            total = w_keep[first.start + j, row, :]
            for k in range(1, n):
                total = total + rs_in[k, j]
            piece_buf[j] = tied3[first.start + j, row, :] * (0.5 * total) / piece_buf[j]
        for k in range(1, n):
            ag_copies[k].start()
        fw_copies[0].start()

    owner_only(me, own_piece)

    def put(index, ref, flip):
        first, row = piece_at(index)
        for j in range(per):
            block = first.start + j
            value = ref[j]
            if flip:
                block = blocks - 1 - block
                value = mirrored(value)
            col = pl.multiple_of(block * LANES, LANES)
            new_basis[row, pl.ds(col, LANES)] = value

    def arrived(k):
        def go():
            ag_copies[k].wait_recv()
            fw_copies[k].start()
            put(source(k), ag_in.at[k], False)
        return go

    def passed_on(k):
        def go():
            fw_copies[k].wait_recv()
            put(source(k), fw_in.at[k], True)
        return go

    for k in range(1, n):
        owner_only(source(k), arrived(k))
    owner_only(me, lambda: put(me, piece_buf, False))
    owner_only(me, passed_on(0))
    for k in range(1, n):
        owner_only(source(k), passed_on(k))

    for k in range(1, n):
        owner_only(peer(k), rs_copies[k].wait_send)
        owner_only(me, ag_copies[k].wait_send)
        owner_only(source(k), fw_copies[k].wait_send)
    owner_only(me, fw_copies[0].wait_send)


def per_device(n, spectra, basis, loadings):
    rank, pixels = basis.shape
    positions = loadings.shape[1]
    blocks = pixels // LANES
    half = blocks // 2
    if n <= half:
        per, row_split = half // n, 1
    else:
        per, row_split = 1, min(n // half, rank // 8)
    rows = rank // row_split
    load_chunks = 8
    pos_chunk = 256
    col_chunk = 256
    pack = LANES // rank
    dma = pltpu.SemaphoreType.DMA
    any_space = pl.BlockSpec(memory_space=pl.ANY)
    vmem = pl.BlockSpec(memory_space=pltpu.VMEM)
    return pl.pallas_call(
        functools.partial(kernel, n, load_chunks, pos_chunk, col_chunk, 4),
        out_shape=(
            jax.ShapeDtypeStruct(loadings.shape, F32),
            jax.ShapeDtypeStruct(basis.shape, F32),
        ),
        in_specs=[any_space] * 3,
        out_specs=(vmem, vmem),
        scratch_shapes=[
            pltpu.VMEM(spectra.shape, F32),
            pltpu.VMEM(spectra.shape, BF16),
            pltpu.VMEM(spectra.shape, BF16),
            pltpu.VMEM((rank, pixels), F32),
            pltpu.VMEM((rank, pixels), F32),
            pltpu.VMEM((rank, positions), F32),
            pltpu.VMEM((blocks, rank, LANES), F32),
            pltpu.VMEM((2 * rank, pixels), BF16),
            pltpu.VMEM((positions // pos_chunk, rank, pos_chunk), F32),
            pltpu.VMEM((positions // pos_chunk, rank, pos_chunk), F32),
            pltpu.VMEM((2 * rank, positions), BF16),
            pltpu.VMEM((half, rank, LANES), F32),
            pltpu.VMEM((half, rank, LANES), F32),
            pltpu.VMEM((half, rank, LANES), F32),
            pltpu.VMEM((n, per, rows, LANES), F32),
            pltpu.VMEM((rank // pack, LANES), F32),
            pltpu.VMEM((n, rank // pack, LANES), F32),
            pltpu.VMEM((per, rows, LANES), F32),
            pltpu.VMEM((n, per, rows, LANES), F32),
            pltpu.VMEM((n, per, rows, LANES), F32),
            dma((load_chunks,)),
            dma((2,)),
            dma((2,)),
            dma((2, positions // pos_chunk)),
            dma((2, half * LANES // col_chunk)),
            dma((n,)), dma((n,)), dma((n,)), dma((n,)),
            dma((n,)), dma((n,)), dma((n,)), dma((n,)),
        ],
        compiler_params=pltpu.CompilerParams(collective_id=0, has_side_effects=True),
        name="nmf_update",
    )(spectra, basis, loadings)


def solution(mesh):
    in_specs = (P(("grp", "scan"), "det"), P("grp", "det"), P("grp", "scan"))
    out_specs = (P("grp", "scan"), P("grp", "det"))
    return jax.shard_map(
        functools.partial(per_device, mesh.shape["scan"]),
        mesh=mesh, in_specs=in_specs, out_specs=out_specs, check_vma=False,
    )
```

```python
import functools

import jax
import jax.numpy as jnp
from jax import lax
from jax.experimental import pallas as pl
from jax.experimental.pallas import tpu as pltpu
from jax.sharding import PartitionSpec as P

HIGHEST = lax.Precision.HIGHEST
MESH = pl.DeviceIdType.MESH
F32 = jnp.float32
BF16 = jnp.bfloat16
LANES = 128


def split(x):
    hi = x.astype(BF16)
    lo = (x - hi.astype(F32)).astype(BF16)
    return hi, lo


def dot_nt(a, b):
    return lax.dot_general(a, b, (((1,), (1,)), ((), ())), preferred_element_type=F32)


def dot_nn(a, b):
    return lax.dot_general(a, b, (((1,), (0,)), ((), ())), preferred_element_type=F32)


def mirrored(x):
    index = (LANES - 1) - lax.broadcasted_iota(jnp.int32, x.shape, 1)
    return jnp.take_along_axis(x, index, axis=1, mode="promise_in_bounds")


def remote(src, dst, send, recv, where):
    return pltpu.make_async_remote_copy(
        src_ref=src, dst_ref=dst, send_sem=send, recv_sem=recv,
        device_id=where, device_id_type=MESH,
    )


def layout(n, rank, pixels):
    half = pixels // LANES // 2
    if n <= half:
        per, row_split = half // n, 1
    else:
        per, row_split = 1, min(n // half, rank // 8)
    return half, per, row_split


def piece_at(index, per, row_split, rows):
    first = index // row_split * per
    row = pl.multiple_of(lax.rem(index, row_split) * rows, 8) if row_split > 1 else 0
    return pl.ds(first, per), pl.ds(row, rows)


def loadings_kernel(
    load_chunks, early, pos_chunk,
    spectra, basis, loadings,
    new_loadings, nl2, s_hi, s_lo, tied3, packed,
    sbuf, own, other, load, tied2, num_out, num_in,
    sp_sem, io_sem, bs_sem, nm_sem,
):
    rank, pixels = basis.shape
    positions = loadings.shape[1]
    blocks = pixels // LANES
    pack = LANES // rank
    partner = {"det": 1 - lax.axis_index("det")}
    barrier = pltpu.get_barrier_semaphore()
    pl.semaphore_signal(barrier, inc=1, device_id=partner, device_id_type=MESH)

    load_rows = positions // load_chunks
    spectra_copies = []
    for i in range(load_chunks):
        part = pl.ds(i * load_rows, load_rows)
        spectra_copies.append(
            pltpu.make_async_copy(spectra.at[part], sbuf.at[part], sp_sem.at[i])
        )
    own_copy = pltpu.make_async_copy(basis, own, io_sem.at[0])
    load_copy = pltpu.make_async_copy(loadings, load, io_sem.at[1])
    basis_copy = remote(basis, other, bs_sem.at[0], bs_sem.at[1], partner)
    for i in range(early):
        spectra_copies[i].start()
    pl.semaphore_wait(barrier, 1)
    basis_copy.start()
    own_copy.start()
    load_copy.start()
    for i in range(early, load_chunks):
        spectra_copies[i].start()

    def divide(i):
        spectra_copies[i].wait()

        @pl.loop(0, load_rows // 16)
        def _(j):
            part = pl.ds(pl.multiple_of(i * load_rows + j * 16, 16), 16)
            hi, lo = split(sbuf[part, :])
            s_hi[part, :] = hi
            s_lo[part, :] = lo

    per_pos = pos_chunk // load_rows
    for i in range(early):
        divide(i)
    own_copy.wait()
    basis_copy.wait()
    for b in range(blocks):
        mine = own[:, b * LANES:(b + 1) * LANES]
        back = blocks - 1 - b
        tied = 0.5 * (mine + mirrored(other[:, back * LANES:(back + 1) * LANES]))
        tied3[b] = tied
        hi, lo = split(tied)
        tied2[:rank, b * LANES:(b + 1) * LANES] = hi
        tied2[rank:, b * LANES:(b + 1) * LANES] = lo

    chunks = positions // pos_chunk
    num_copies = [
        remote(num_out.at[i], num_in.at[i], nm_sem.at[0, i], nm_sem.at[1, i], partner)
        for i in range(chunks)
    ]

    def products(i):
        for j in range(max(i * per_pos, early), (i + 1) * per_pos):
            divide(j)
        part = pl.ds(i * pos_chunk, pos_chunk)
        both = dot_nt(tied2[...], s_hi[part, :])
        low = dot_nt(tied2[:rank, :], s_lo[part, :])
        num_out[i] = both[:rank] + (both[rank:] + low)
        num_copies[i].start()

    def update(i):
        num_copies[i].wait()
        cols = slice(i * pos_chunk, (i + 1) * pos_chunk)
        fresh = load[:, cols] * (num_out[i] + num_in[i]) / weighted[:, cols]
        new_loadings[:, cols] = fresh
        hi, lo = split(fresh)
        nl2[:rank, cols] = hi
        nl2[rank:, cols] = lo
        return dot_nt(nl2[:, cols], nl2[:, cols])

    products(0)
    squares = dot_nt(tied2[...], tied2[...])
    gram = 2.0 * (
        squares[:rank, :rank] + (squares[:rank, rank:] + squares[rank:, :rank])
    )
    load_copy.wait()
    weighted = jnp.dot(gram, load[...], precision=HIGHEST, preferred_element_type=F32)
    squares = 0.0
    for i in range(1, chunks):
        products(i)
        if i > 1:
            squares = squares + update(i - 2)
    for i in range(max(chunks - 2, 0), chunks):
        squares = squares + update(i)
    cross = squares[:rank, :rank] + (squares[:rank, rank:] + squares[rank:, :rank])
    packed[...] = jnp.concatenate(
        [cross[i * (rank // pack):(i + 1) * (rank // pack)] for i in range(pack)], axis=1
    )


def basis_kernel(
    n, col_chunk, wait_at,
    nl2, s_hi, s_lo, tied3, packed,
    piece_buf, ag_in, fw_in,
    w_keep, w_out, w_in, rs_in, cr_out, cr_in,
    io_sem, w_sem, rs_send, rs_recv, cr_send, cr_recv,
    ag_send, ag_recv, fw_send, fw_recv,
):
    blocks, rank, _ = tied3.shape
    half, per, row_split = layout(n, rank, blocks * LANES)
    owners = half // per * row_split
    rows = rank // row_split
    pack = LANES // rank
    me = lax.axis_index("scan")
    partner = {"det": 1 - lax.axis_index("det")}

    def peer(k):
        return lax.rem(me + k, n)

    def source(k):
        return lax.rem(me + n - k, n)

    def owner_only(index, fn):
        if owners == n:
            fn()
        else:
            pl.when(index < owners)(fn)

    barrier = pltpu.get_barrier_semaphore()
    for k in range(1, n):
        pl.semaphore_signal(barrier, inc=1, device_id={"scan": peer(k)}, device_id_type=MESH)
    pl.semaphore_signal(barrier, inc=1, device_id=partner, device_id_type=MESH)
    keep = pltpu.make_async_copy(packed, cr_out, io_sem.at[0])
    keep.start()

    def sums(cols):
        both = dot_nn(nl2[...], s_hi[:, cols])
        low = dot_nn(nl2[:rank, :], s_lo[:, cols])
        return both[:rank] + (both[rank:] + low)

    step = col_chunk // LANES
    count = half // step
    w_copies = []
    for i in range(count):
        part = pl.ds(i * step, step)
        w_copies.append(
            remote(w_out.at[part], w_in.at[part], w_sem.at[0, i], w_sem.at[1, i], partner)
        )
    cr_copies = [None]
    for k in range(1, n):
        cr_copies.append(
            remote(cr_out, cr_in.at[k], cr_send.at[k], cr_recv.at[k], {"scan": peer(k)})
        )
    for i in range(count):
        first = half + i * step
        value = sums(slice(first * LANES, (first + step) * LANES))
        for j in range(step):
            w_out[i * step + j] = value[:, j * LANES:(j + 1) * LANES]
    keep.wait()

    def meet():
        pl.semaphore_wait(barrier, n)
        for copy in w_copies:
            copy.start()
        for k in range(1, n):
            cr_copies[k].start()

    for i in range(count):
        if i == wait_at:
            meet()
        value = sums(slice(i * col_chunk, (i + 1) * col_chunk))
        for j in range(step):
            w_keep[i * step + j] = value[:, j * LANES:(j + 1) * LANES]
    if wait_at >= count:
        meet()
    for copy in w_copies:
        copy.wait()
    for b in range(half):
        w_keep[b] = w_keep[b] + mirrored(w_in[half - 1 - b])

    rs_copies = [None]
    for k in range(1, n):
        rs_copies.append(
            remote(
                w_keep.at[piece_at(peer(k), per, row_split, rows)], rs_in.at[k],
                rs_send.at[k], rs_recv.at[k], {"scan": peer(k)},
            )
        )
        owner_only(peer(k), rs_copies[k].start)

    for k in range(1, n):
        cr_copies[k].wait()
    total = cr_out[...]
    for k in range(1, n):
        total = total + cr_in[k]
    cross = jnp.concatenate(
        [total[:, i * rank:(i + 1) * rank] for i in range(pack)], axis=0
    )

    ag_copies = [None]
    for k in range(1, n):
        ag_copies.append(
            remote(piece_buf, ag_in.at[k], ag_send.at[k], ag_recv.at[k], {"scan": peer(k)})
        )
    fw_copies = [remote(piece_buf, fw_in.at[0], fw_send.at[0], fw_recv.at[0], partner)]
    for k in range(1, n):
        fw_copies.append(
            remote(ag_in.at[k], fw_in.at[k], fw_send.at[k], fw_recv.at[k], partner)
        )

    def own_piece():
        first, row = piece_at(me, per, row_split, rows)
        for j in range(per):
            weights = jnp.dot(
                cross, tied3[first.start + j], precision=HIGHEST, preferred_element_type=F32
            )
            if row_split > 1:
                piece_buf[0] = weights[:rows]
                for i in range(1, row_split):
                    @pl.when(lax.rem(me, row_split) == i)
                    def _():
                        piece_buf[0] = weights[i * rows:(i + 1) * rows]
            else:
                piece_buf[j] = weights
        for k in range(1, n):
            rs_copies[k].wait_recv()
        for j in range(per):
            total = w_keep[first.start + j, row, :]
            for k in range(1, n):
                total = total + rs_in[k, j]
            piece_buf[j] = tied3[first.start + j, row, :] * (0.5 * total) / piece_buf[j]
        for k in range(1, n):
            ag_copies[k].start()
        fw_copies[0].start()

    owner_only(me, own_piece)

    def arrived(k):
        def go():
            ag_copies[k].wait_recv()
            fw_copies[k].start()
        return go

    for k in range(1, n):
        owner_only(source(k), arrived(k))
    owner_only(me, fw_copies[0].wait)
    for k in range(1, n):
        owner_only(source(k), fw_copies[k].wait)
    for k in range(1, n):
        owner_only(peer(k), rs_copies[k].wait_send)
        owner_only(me, ag_copies[k].wait_send)


def output_kernel(
    n, fresh, piece_buf, ag_in, fw_in, new_loadings, new_basis, nb, io_sem
):
    rank, pixels = nb.shape
    half, per, row_split = layout(n, rank, pixels)
    owners = half // per * row_split
    rows = rank // row_split
    me = lax.axis_index("scan")
    first_copy = pltpu.make_async_copy(fresh, new_loadings, io_sem.at[0])
    first_copy.start()

    def put(index, ref, flip):
        first, row = piece_at(index, per, row_split, rows)
        for j in range(per):
            block = first.start + j
            value = ref[j]
            if flip:
                block = pixels // LANES - 1 - block
                value = mirrored(value)
            nb[row, pl.ds(pl.multiple_of(block * LANES, LANES), LANES)] = value

    for k in range(n):
        index = lax.rem(me + n - k, n)

        def go():
            put(index, piece_buf if k == 0 else ag_in.at[k], False)
            put(index, fw_in.at[k], True)

        if owners == n:
            go()
        else:
            pl.when(index < owners)(go)
    second_copy = pltpu.make_async_copy(nb, new_basis, io_sem.at[1])
    second_copy.start()
    first_copy.wait()
    second_copy.wait()


def per_device(n, spectra, basis, loadings):
    rank, pixels = basis.shape
    positions = loadings.shape[1]
    blocks = pixels // LANES
    half, per, row_split = layout(n, rank, pixels)
    rows = rank // row_split
    load_chunks = 8
    pos_chunk = positions // 4
    col_chunk = 2 * LANES
    pack = LANES // rank
    dma = pltpu.SemaphoreType.DMA
    any_space = pl.BlockSpec(memory_space=pl.ANY)
    vmem = pl.BlockSpec(memory_space=pltpu.VMEM)
    fresh, nl2, s_hi, s_lo, tied3, packed = pl.pallas_call(
        functools.partial(loadings_kernel, load_chunks, 4, pos_chunk),
        out_shape=(
            pltpu.VMEM(loadings.shape, F32),
            pltpu.VMEM((2 * rank, positions), BF16),
            pltpu.VMEM(spectra.shape, BF16),
            pltpu.VMEM(spectra.shape, BF16),
            pltpu.VMEM((blocks, rank, LANES), F32),
            pltpu.VMEM((rank // pack, LANES), F32),
        ),
        in_specs=[pl.BlockSpec(memory_space=pltpu.HBM)] * 3,
        out_specs=(vmem,) * 6,
        scratch_shapes=[
            pltpu.VMEM(spectra.shape, F32),
            pltpu.VMEM((rank, pixels), F32),
            pltpu.VMEM((rank, pixels), F32),
            pltpu.VMEM((rank, positions), F32),
            pltpu.VMEM((2 * rank, pixels), BF16),
            pltpu.VMEM((positions // pos_chunk, rank, pos_chunk), F32),
            pltpu.VMEM((positions // pos_chunk, rank, pos_chunk), F32),
            dma((load_chunks,)),
            dma((2,)),
            dma((2,)),
            dma((2, positions // pos_chunk)),
        ],
        compiler_params=pltpu.CompilerParams(
            collective_id=0, has_side_effects=True, vmem_limit_bytes=40 << 20
        ),
        name="loadings_update",
    )(spectra, basis, loadings)
    pieces = pl.pallas_call(
        functools.partial(basis_kernel, n, col_chunk, 3),
        out_shape=(
            pltpu.VMEM((per, rows, LANES), F32),
            pltpu.VMEM((n, per, rows, LANES), F32),
            pltpu.VMEM((n, per, rows, LANES), F32),
        ),
        in_specs=[vmem] * 5,
        out_specs=(vmem,) * 3,
        scratch_shapes=[
            pltpu.VMEM((half, rank, LANES), F32),
            pltpu.VMEM((half, rank, LANES), F32),
            pltpu.VMEM((half, rank, LANES), F32),
            pltpu.VMEM((n, per, rows, LANES), F32),
            pltpu.VMEM((rank // pack, LANES), F32),
            pltpu.VMEM((n, rank // pack, LANES), F32),
            dma((1,)),
            dma((2, half * LANES // col_chunk)),
            dma((n,)), dma((n,)), dma((n,)), dma((n,)),
            dma((n,)), dma((n,)), dma((n,)), dma((n,)),
        ],
        compiler_params=pltpu.CompilerParams(
            collective_id=1, has_side_effects=True, vmem_limit_bytes=32 << 20
        ),
        name="basis_update",
    )(nl2, s_hi, s_lo, tied3, packed)
    return pl.pallas_call(
        functools.partial(output_kernel, n),
        out_shape=(
            jax.ShapeDtypeStruct(loadings.shape, F32),
            jax.ShapeDtypeStruct(basis.shape, F32),
        ),
        in_specs=[vmem] * 4,
        out_specs=(any_space,) * 2,
        scratch_shapes=[pltpu.VMEM((rank, pixels), F32), dma((2,))],
        compiler_params=pltpu.CompilerParams(vmem_limit_bytes=8 << 20),
        name="write_out",
    )(fresh, *pieces)


def solution(mesh):
    in_specs = (P(("grp", "scan"), "det"), P("grp", "det"), P("grp", "scan"))
    out_specs = (P("grp", "scan"), P("grp", "det"))
    return jax.shard_map(
        functools.partial(per_device, mesh.shape["scan"]),
        mesh=mesh, in_specs=in_specs, out_specs=out_specs, check_vma=False,
    )
```

```python
import functools

import jax
import jax.numpy as jnp
from jax import lax
from jax.experimental import pallas as pl
from jax.experimental.pallas import tpu as pltpu
from jax.sharding import PartitionSpec as P

HIGHEST = lax.Precision.HIGHEST
MESH = pl.DeviceIdType.MESH
F32 = jnp.float32
BF16 = jnp.bfloat16
LANES = 128


def split(x):
    hi = x.astype(BF16)
    lo = (x - hi.astype(F32)).astype(BF16)
    return hi, lo


def dot_nt(a, b):
    return lax.dot_general(a, b, (((1,), (1,)), ((), ())), preferred_element_type=F32)


def dot_nn(a, b):
    return lax.dot_general(a, b, (((1,), (0,)), ((), ())), preferred_element_type=F32)


def mirrored(x):
    index = (LANES - 1) - lax.broadcasted_iota(jnp.int32, x.shape, 1)
    return jnp.take_along_axis(x, index, axis=1, mode="promise_in_bounds")


def remote(src, dst, send, recv, where):
    return pltpu.make_async_remote_copy(
        src_ref=src, dst_ref=dst, send_sem=send, recv_sem=recv,
        device_id=where, device_id_type=MESH,
    )


def layout(n, rank, pixels):
    half = pixels // LANES // 2
    if n <= half:
        per, row_split = half // n, 1
    else:
        per, row_split = 1, min(n // half, rank // 8)
    return half, per, row_split


def piece_at(index, per, row_split, rows):
    first = index // row_split * per
    row = pl.multiple_of(lax.rem(index, row_split) * rows, 8) if row_split > 1 else 0
    return pl.ds(first, per), pl.ds(row, rows)


def tie_kernel(
    load_chunks, early,
    spectra, basis, loadings,
    s_hi, s_lo, tied3, tied2, load, weighted,
    sbuf, own, other, sp_sem, io_sem, bs_sem,
):
    rank, pixels = basis.shape
    positions = loadings.shape[1]
    blocks = pixels // LANES
    partner = {"det": 1 - lax.axis_index("det")}
    barrier = pltpu.get_barrier_semaphore()
    pl.semaphore_signal(barrier, inc=1, device_id=partner, device_id_type=MESH)

    load_rows = positions // load_chunks
    spectra_copies = []
    for i in range(load_chunks):
        part = pl.ds(i * load_rows, load_rows)
        spectra_copies.append(
            pltpu.make_async_copy(spectra.at[part], sbuf.at[part], sp_sem.at[i])
        )
    own_copy = pltpu.make_async_copy(basis, own, io_sem.at[0])
    load_copy = pltpu.make_async_copy(loadings, load, io_sem.at[1])
    basis_copy = remote(basis, other, bs_sem.at[0], bs_sem.at[1], partner)
    for i in range(early):
        spectra_copies[i].start()
    pl.semaphore_wait(barrier, 1)
    basis_copy.start()
    own_copy.start()
    load_copy.start()
    for i in range(early, load_chunks):
        spectra_copies[i].start()

    def divide(i):
        spectra_copies[i].wait()

        @pl.loop(0, load_rows // 16, unroll=True)
        def _(j):
            part = pl.ds(pl.multiple_of(i * load_rows + j * 16, 16), 16)
            hi, lo = split(sbuf[part, :])
            s_hi[part, :] = hi
            s_lo[part, :] = lo

    for i in range(early):
        divide(i)
    own_copy.wait()
    basis_copy.wait()
    for b in range(blocks):
        mine = own[:, b * LANES:(b + 1) * LANES]
        back = blocks - 1 - b
        tied = 0.5 * (mine + mirrored(other[:, back * LANES:(back + 1) * LANES]))
        tied3[b] = tied
        hi, lo = split(tied)
        tied2[:rank, b * LANES:(b + 1) * LANES] = hi
        tied2[rank:, b * LANES:(b + 1) * LANES] = lo
    squares = dot_nt(tied2[...], tied2[...])
    gram = 2.0 * (
        squares[:rank, :rank] + (squares[:rank, rank:] + squares[rank:, :rank])
    )
    load_copy.wait()
    weighted[...] = jnp.dot(
        gram, load[...], precision=HIGHEST, preferred_element_type=F32
    )
    for i in range(early, load_chunks):
        divide(i)


def update_kernel(
    n, pos_chunk, col_chunk, wait_at,
    s_hi, s_lo, tied3, tied2, load, weighted,
    new_loadings, piece_buf, ag_in, fw_in,
    nl2, num_out, num_in, w_keep, w_out, w_in, rs_in, cr_out, cr_in,
    nm_sem, w_sem, rs_send, rs_recv, cr_send, cr_recv,
    ag_send, ag_recv, fw_send, fw_recv,
):
    blocks, rank, _ = tied3.shape
    half, per, row_split = layout(n, rank, blocks * LANES)
    owners = half // per * row_split
    rows = rank // row_split
    pack = LANES // rank
    me = lax.axis_index("scan")
    partner = {"det": 1 - lax.axis_index("det")}

    def peer(k):
        return lax.rem(me + k, n)

    def source(k):
        return lax.rem(me + n - k, n)

    def owner_only(index, fn):
        if owners == n:
            fn()
        else:
            pl.when(index < owners)(fn)

    barrier = pltpu.get_barrier_semaphore()
    for k in range(1, n):
        pl.semaphore_signal(barrier, inc=1, device_id={"scan": peer(k)}, device_id_type=MESH)
    pl.semaphore_signal(barrier, inc=1, device_id=partner, device_id_type=MESH)
    positions = load.shape[1]
    chunks = positions // pos_chunk
    num_copies = [
        remote(num_out.at[i], num_in.at[i], nm_sem.at[0, i], nm_sem.at[1, i], partner)
        for i in range(chunks)
    ]

    def products(i):
        part = pl.ds(i * pos_chunk, pos_chunk)
        both = dot_nt(tied2[...], s_hi[part, :])
        low = dot_nt(tied2[:rank, :], s_lo[part, :])
        num_out[i] = both[:rank] + (both[rank:] + low)

    def update(i):
        num_copies[i].wait()
        cols = slice(i * pos_chunk, (i + 1) * pos_chunk)
        fresh = load[:, cols] * (num_out[i] + num_in[i]) / weighted[:, cols]
        new_loadings[:, cols] = fresh
        hi, lo = split(fresh)
        nl2[:rank, cols] = hi
        nl2[rank:, cols] = lo

    for i in range(chunks):
        products(i)
        if i == wait_at:
            pl.semaphore_wait(barrier, n)
            for j in range(i):
                num_copies[j].start()
        if i >= wait_at:
            num_copies[i].start()
    for i in range(chunks):
        update(i)

    def sums(cols):
        both = dot_nn(nl2[...], s_hi[:, cols])
        low = dot_nn(nl2[:rank, :], s_lo[:, cols])
        return both[:rank] + (both[rank:] + low)

    step = col_chunk // LANES
    count = half // step
    w_copies = []
    for i in range(count):
        part = pl.ds(i * step, step)
        w_copies.append(
            remote(w_out.at[part], w_in.at[part], w_sem.at[0, i], w_sem.at[1, i], partner)
        )
    cr_copies = [None]
    for k in range(1, n):
        cr_copies.append(
            remote(cr_out, cr_in.at[k], cr_send.at[k], cr_recv.at[k], {"scan": peer(k)})
        )
    for i in range(count):
        first = half + i * step
        value = sums(slice(first * LANES, (first + step) * LANES))
        for j in range(step):
            w_out[i * step + j] = value[:, j * LANES:(j + 1) * LANES]
        w_copies[i].start()
    squares = dot_nt(nl2[...], nl2[...])
    cross = squares[:rank, :rank] + (squares[:rank, rank:] + squares[rank:, :rank])
    cr_out[...] = jnp.concatenate(
        [cross[i * (rank // pack):(i + 1) * (rank // pack)] for i in range(pack)], axis=1
    )
    for k in range(1, n):
        cr_copies[k].start()

    for i in range(count):
        value = sums(slice(i * col_chunk, (i + 1) * col_chunk))
        for j in range(step):
            w_keep[i * step + j] = value[:, j * LANES:(j + 1) * LANES]
    for copy in w_copies:
        copy.wait()
    for b in range(half):
        w_keep[b] = w_keep[b] + mirrored(w_in[half - 1 - b])

    rs_copies = [None]
    for k in range(1, n):
        rs_copies.append(
            remote(
                w_keep.at[piece_at(peer(k), per, row_split, rows)], rs_in.at[k],
                rs_send.at[k], rs_recv.at[k], {"scan": peer(k)},
            )
        )
        owner_only(peer(k), rs_copies[k].start)

    for k in range(1, n):
        cr_copies[k].wait()
    total = cr_out[...]
    for k in range(1, n):
        total = total + cr_in[k]
    cross = jnp.concatenate(
        [total[:, i * rank:(i + 1) * rank] for i in range(pack)], axis=0
    )

    ag_copies = [None]
    for k in range(1, n):
        ag_copies.append(
            remote(piece_buf, ag_in.at[k], ag_send.at[k], ag_recv.at[k], {"scan": peer(k)})
        )
    fw_copies = [remote(piece_buf, fw_in.at[0], fw_send.at[0], fw_recv.at[0], partner)]
    for k in range(1, n):
        fw_copies.append(
            remote(ag_in.at[k], fw_in.at[k], fw_send.at[k], fw_recv.at[k], partner)
        )

    def own_piece():
        first, row = piece_at(me, per, row_split, rows)
        for j in range(per):
            weights = jnp.dot(
                cross, tied3[first.start + j], precision=HIGHEST, preferred_element_type=F32
            )
            if row_split > 1:
                piece_buf[0] = weights[:rows]
                for i in range(1, row_split):
                    @pl.when(lax.rem(me, row_split) == i)
                    def _():
                        piece_buf[0] = weights[i * rows:(i + 1) * rows]
            else:
                piece_buf[j] = weights
        for k in range(1, n):
            rs_copies[k].wait_recv()
        for j in range(per):
            total = w_keep[first.start + j, row, :]
            for k in range(1, n):
                total = total + rs_in[k, j]
            piece_buf[j] = tied3[first.start + j, row, :] * (0.5 * total) / piece_buf[j]
        for k in range(1, n):
            ag_copies[k].start()
        fw_copies[0].start()

    owner_only(me, own_piece)

    def arrived(k):
        def go():
            ag_copies[k].wait_recv()
            fw_copies[k].start()
        return go

    for k in range(1, n):
        owner_only(source(k), arrived(k))
    owner_only(me, fw_copies[0].wait)
    for k in range(1, n):
        owner_only(source(k), fw_copies[k].wait)
    for k in range(1, n):
        owner_only(peer(k), rs_copies[k].wait_send)
        owner_only(me, ag_copies[k].wait_send)


def output_kernel(
    n, fresh, piece_buf, ag_in, fw_in, new_loadings, new_basis, nb, io_sem
):
    rank, pixels = nb.shape
    half, per, row_split = layout(n, rank, pixels)
    owners = half // per * row_split
    rows = rank // row_split
    me = lax.axis_index("scan")
    first_copy = pltpu.make_async_copy(fresh, new_loadings, io_sem.at[0])
    first_copy.start()

    def put(index, ref, flip):
        first, row = piece_at(index, per, row_split, rows)
        for j in range(per):
            block = first.start + j
            value = ref[j]
            if flip:
                block = pixels // LANES - 1 - block
                value = mirrored(value)
            nb[row, pl.ds(pl.multiple_of(block * LANES, LANES), LANES)] = value

    for k in range(n):
        index = lax.rem(me + n - k, n)

        def go():
            put(index, piece_buf if k == 0 else ag_in.at[k], False)
            put(index, fw_in.at[k], True)

        if owners == n:
            go()
        else:
            pl.when(index < owners)(go)
    second_copy = pltpu.make_async_copy(nb, new_basis, io_sem.at[1])
    second_copy.start()
    first_copy.wait()
    second_copy.wait()


def per_device(n, spectra, basis, loadings):
    rank, pixels = basis.shape
    positions = loadings.shape[1]
    blocks = pixels // LANES
    half, per, row_split = layout(n, rank, pixels)
    rows = rank // row_split
    load_chunks = 8
    pos_chunk = positions // 4
    col_chunk = 2 * LANES
    pack = LANES // rank
    dma = pltpu.SemaphoreType.DMA
    any_space = pl.BlockSpec(memory_space=pl.ANY)
    vmem = pl.BlockSpec(memory_space=pltpu.VMEM)
    hbm = pl.BlockSpec(memory_space=pltpu.HBM)
    inputs = [pltpu.with_memory_space_constraint(x, pltpu.HBM) for x in (spectra, basis, loadings)]
    parts = pl.pallas_call(
        functools.partial(tie_kernel, load_chunks, 4),
        out_shape=(
            pltpu.VMEM(spectra.shape, BF16),
            pltpu.VMEM(spectra.shape, BF16),
            pltpu.VMEM((blocks, rank, LANES), F32),
            pltpu.VMEM((2 * rank, pixels), BF16),
            pltpu.VMEM((rank, positions), F32),
            pltpu.VMEM((rank, positions), F32),
        ),
        in_specs=[hbm] * 3,
        out_specs=(vmem,) * 6,
        scratch_shapes=[
            pltpu.VMEM(spectra.shape, F32),
            pltpu.VMEM((rank, pixels), F32),
            pltpu.VMEM((rank, pixels), F32),
            dma((load_chunks,)),
            dma((2,)),
            dma((2,)),
        ],
        compiler_params=pltpu.CompilerParams(
            collective_id=0, has_side_effects=True, vmem_limit_bytes=32 << 20
        ),
        name="tie_and_split",
    )(*inputs)
    outs = pl.pallas_call(
        functools.partial(update_kernel, n, pos_chunk, col_chunk, 2),
        out_shape=(
            pltpu.VMEM(loadings.shape, F32),
            pltpu.VMEM((per, rows, LANES), F32),
            pltpu.VMEM((n, per, rows, LANES), F32),
            pltpu.VMEM((n, per, rows, LANES), F32),
        ),
        in_specs=[vmem] * 6,
        out_specs=(vmem,) * 4,
        scratch_shapes=[
            pltpu.VMEM((2 * rank, positions), BF16),
            pltpu.VMEM((positions // pos_chunk, rank, pos_chunk), F32),
            pltpu.VMEM((positions // pos_chunk, rank, pos_chunk), F32),
            pltpu.VMEM((half, rank, LANES), F32),
            pltpu.VMEM((half, rank, LANES), F32),
            pltpu.VMEM((half, rank, LANES), F32),
            pltpu.VMEM((n, per, rows, LANES), F32),
            pltpu.VMEM((rank // pack, LANES), F32),
            pltpu.VMEM((n, rank // pack, LANES), F32),
            dma((2, positions // pos_chunk)),
            dma((2, half * LANES // col_chunk)),
            dma((n,)), dma((n,)), dma((n,)), dma((n,)),
            dma((n,)), dma((n,)), dma((n,)), dma((n,)),
        ],
        compiler_params=pltpu.CompilerParams(
            collective_id=1, has_side_effects=True, vmem_limit_bytes=32 << 20
        ),
        name="update",
    )(*parts)
    return pl.pallas_call(
        functools.partial(output_kernel, n),
        out_shape=(
            jax.ShapeDtypeStruct(loadings.shape, F32),
            jax.ShapeDtypeStruct(basis.shape, F32),
        ),
        in_specs=[vmem] * 4,
        out_specs=(any_space,) * 2,
        scratch_shapes=[pltpu.VMEM((rank, pixels), F32), dma((2,))],
        compiler_params=pltpu.CompilerParams(vmem_limit_bytes=8 << 20),
        name="write_out",
    )(*outs)


def solution(mesh):
    in_specs = (P(("grp", "scan"), "det"), P("grp", "det"), P("grp", "scan"))
    out_specs = (P("grp", "scan"), P("grp", "det"))
    return jax.shard_map(
        functools.partial(per_device, mesh.shape["scan"]),
        mesh=mesh, in_specs=in_specs, out_specs=out_specs, check_vma=False,
    )
```

```python
import functools

import jax
import jax.numpy as jnp
from jax import lax
from jax.experimental import pallas as pl
from jax.experimental.pallas import tpu as pltpu
from jax.sharding import PartitionSpec as P

HIGHEST = lax.Precision.HIGHEST
MESH = pl.DeviceIdType.MESH
F32 = jnp.float32
BF16 = jnp.bfloat16
LANES = 128


def split(x):
    hi = x.astype(BF16)
    lo = (x - hi.astype(F32)).astype(BF16)
    return hi, lo


def dot_nt(a, b):
    return lax.dot_general(a, b, (((1,), (1,)), ((), ())), preferred_element_type=F32)


def dot_nn(a, b):
    return lax.dot_general(a, b, (((1,), (0,)), ((), ())), preferred_element_type=F32)


def mirrored(x):
    index = (LANES - 1) - lax.broadcasted_iota(jnp.int32, x.shape, 1)
    return jnp.take_along_axis(x, index, axis=1, mode="promise_in_bounds")


def remote(src, dst, send, recv, where):
    return pltpu.make_async_remote_copy(
        src_ref=src, dst_ref=dst, send_sem=send, recv_sem=recv,
        device_id=where, device_id_type=MESH,
    )


def layout(n, rank, pixels):
    half = pixels // LANES // 2
    if n <= half:
        per, row_split = half // n, 1
    else:
        per, row_split = 1, min(n // half, rank // 8)
    return half, per, row_split


def piece_at(index, per, row_split, rows):
    first = index // row_split * per
    row = pl.multiple_of(lax.rem(index, row_split) * rows, 8) if row_split > 1 else 0
    return pl.ds(first, per), pl.ds(row, rows)


def tie_kernel(
    load_chunks, early,
    spectra, basis, loadings,
    s_hi, s_lo, tied3, tied2, load, weighted,
    sbuf, own, other, sp_sem, io_sem, bs_sem,
):
    rank, pixels = basis.shape
    positions = loadings.shape[1]
    blocks = pixels // LANES
    partner = {"det": 1 - lax.axis_index("det")}
    barrier = pltpu.get_barrier_semaphore()
    pl.semaphore_signal(barrier, inc=1, device_id=partner, device_id_type=MESH)

    load_rows = positions // load_chunks
    spectra_copies = []
    for i in range(load_chunks):
        part = pl.ds(i * load_rows, load_rows)
        spectra_copies.append(
            pltpu.make_async_copy(spectra.at[part], sbuf.at[part], sp_sem.at[i])
        )
    own_copy = pltpu.make_async_copy(basis, own, io_sem.at[0])
    load_copy = pltpu.make_async_copy(loadings, load, io_sem.at[1])
    basis_copy = remote(basis, other, bs_sem.at[0], bs_sem.at[1], partner)
    for i in range(early):
        spectra_copies[i].start()
    pl.semaphore_wait(barrier, 1)
    basis_copy.start()
    own_copy.start()
    load_copy.start()
    for i in range(early, load_chunks):
        spectra_copies[i].start()

    def divide(i):
        spectra_copies[i].wait()

        @pl.loop(0, load_rows // 16, unroll=True)
        def _(j):
            part = pl.ds(pl.multiple_of(i * load_rows + j * 16, 16), 16)
            hi, lo = split(sbuf[part, :])
            s_hi[part, :] = hi
            s_lo[part, :] = lo

    for i in range(early):
        divide(i)
    own_copy.wait()
    basis_copy.wait()
    for b in range(blocks):
        mine = own[:, b * LANES:(b + 1) * LANES]
        back = blocks - 1 - b
        tied = 0.5 * (mine + mirrored(other[:, back * LANES:(back + 1) * LANES]))
        tied3[b] = tied
        hi, lo = split(tied)
        tied2[:rank, b * LANES:(b + 1) * LANES] = hi
        tied2[rank:, b * LANES:(b + 1) * LANES] = lo
    squares = dot_nt(tied2[...], tied2[...])
    gram = 2.0 * (
        squares[:rank, :rank] + (squares[:rank, rank:] + squares[rank:, :rank])
    )
    load_copy.wait()
    weighted[...] = jnp.dot(
        gram, load[...], precision=HIGHEST, preferred_element_type=F32
    )
    for i in range(early, load_chunks):
        divide(i)


def update_kernel(
    n, pos_chunk, col_chunk, wait_at,
    s_hi, s_lo, tied3, tied2, load, weighted,
    new_loadings, piece_buf, ag_in, fw_in,
    nl2, num_out, num_in, w_keep, w_out, w_in, rs_in, cr_out, cr_in,
    nm_sem, w_sem, rs_send, rs_recv, cr_send, cr_recv,
    ag_send, ag_recv, fw_send, fw_recv,
):
    blocks, rank, _ = tied3.shape
    half, per, row_split = layout(n, rank, blocks * LANES)
    owners = half // per * row_split
    rows = rank // row_split
    pack = LANES // rank
    me = lax.axis_index("scan")
    partner = {"det": 1 - lax.axis_index("det")}

    def peer(k):
        return lax.rem(me + k, n)

    def source(k):
        return lax.rem(me + n - k, n)

    def owner_only(index, fn):
        if owners == n:
            fn()
        else:
            pl.when(index < owners)(fn)

    barrier = pltpu.get_barrier_semaphore()
    for k in range(1, n):
        pl.semaphore_signal(barrier, inc=1, device_id={"scan": peer(k)}, device_id_type=MESH)
    pl.semaphore_signal(barrier, inc=1, device_id=partner, device_id_type=MESH)
    for k in range(1, n):
        pl.semaphore_signal(
            barrier, inc=1, device_id={"scan": peer(k), **partner}, device_id_type=MESH
        )
    positions = load.shape[1]
    chunks = positions // pos_chunk
    num_copies = [
        remote(num_out.at[i], num_in.at[i], nm_sem.at[0, i], nm_sem.at[1, i], partner)
        for i in range(chunks)
    ]

    def products(i):
        part = pl.ds(i * pos_chunk, pos_chunk)
        both = dot_nt(s_hi[part, :], tied2[...])
        low = dot_nt(s_lo[part, :], tied2[:rank, :])
        num_out[i] = (both[:, :rank] + (both[:, rank:] + low)).T

    def update(i):
        num_copies[i].wait()
        cols = slice(i * pos_chunk, (i + 1) * pos_chunk)
        fresh = load[:, cols] * (num_out[i] + num_in[i]) / weighted[:, cols]
        new_loadings[:, cols] = fresh
        hi, lo = split(fresh)
        nl2[:rank, cols] = hi
        nl2[rank:, cols] = lo

    for i in range(chunks):
        products(i)
        if i == wait_at:
            pl.semaphore_wait(barrier, 2 * n - 1)
            for j in range(i):
                num_copies[j].start()
        if i >= wait_at:
            num_copies[i].start()
    for i in range(chunks):
        update(i)

    def sums(cols):
        both = dot_nn(nl2[...], s_hi[:, cols])
        low = dot_nn(nl2[:rank, :], s_lo[:, cols])
        return both[:rank] + (both[rank:] + low)

    step = col_chunk // LANES
    count = half // step
    w_copies = []
    for i in range(count):
        part = pl.ds(i * step, step)
        w_copies.append(
            remote(w_out.at[part], w_in.at[part], w_sem.at[0, i], w_sem.at[1, i], partner)
        )
    cr_copies = [None]
    for k in range(1, n):
        cr_copies.append(
            remote(cr_out, cr_in.at[k], cr_send.at[k], cr_recv.at[k], {"scan": peer(k)})
        )
    for i in range(count):
        first = half + i * step
        value = sums(slice(first * LANES, (first + step) * LANES))
        for j in range(step):
            w_out[i * step + j] = value[:, j * LANES:(j + 1) * LANES]
        w_copies[i].start()
    squares = dot_nt(nl2[...], nl2[...])
    cross = squares[:rank, :rank] + (squares[:rank, rank:] + squares[rank:, :rank])
    cr_out[...] = jnp.concatenate(
        [cross[i * (rank // pack):(i + 1) * (rank // pack)] for i in range(pack)], axis=1
    )
    for k in range(1, n):
        cr_copies[k].start()

    for i in range(count):
        value = sums(slice(i * col_chunk, (i + 1) * col_chunk))
        for j in range(step):
            w_keep[i * step + j] = value[:, j * LANES:(j + 1) * LANES]
    for copy in w_copies:
        copy.wait()
    for b in range(half):
        w_keep[b] = w_keep[b] + mirrored(w_in[half - 1 - b])

    rs_copies = [None]
    for k in range(1, n):
        rs_copies.append(
            remote(
                w_keep.at[piece_at(peer(k), per, row_split, rows)], rs_in.at[k],
                rs_send.at[k], rs_recv.at[k], {"scan": peer(k)},
            )
        )
        owner_only(peer(k), rs_copies[k].start)

    for k in range(1, n):
        cr_copies[k].wait()
    total = cr_out[...]
    for k in range(1, n):
        total = total + cr_in[k]
    cross = jnp.concatenate(
        [total[:, i * rank:(i + 1) * rank] for i in range(pack)], axis=0
    )

    ag_copies = [None]
    for k in range(1, n):
        ag_copies.append(
            remote(piece_buf, ag_in.at[k], ag_send.at[k], ag_recv.at[k], {"scan": peer(k)})
        )
    fw_copies = [remote(piece_buf, fw_in.at[0], fw_send.at[0], fw_recv.at[0], partner)]
    for k in range(1, n):
        fw_copies.append(
            remote(
                piece_buf, fw_in.at[k], fw_send.at[k], fw_recv.at[k],
                {"scan": peer(k), **partner},
            )
        )

    def own_piece():
        first, row = piece_at(me, per, row_split, rows)
        for j in range(per):
            weights = jnp.dot(
                cross, tied3[first.start + j], precision=HIGHEST, preferred_element_type=F32
            )
            if row_split > 1:
                piece_buf[0] = weights[:rows]
                for i in range(1, row_split):
                    @pl.when(lax.rem(me, row_split) == i)
                    def _():
                        piece_buf[0] = weights[i * rows:(i + 1) * rows]
            else:
                piece_buf[j] = weights
        for k in range(1, n):
            rs_copies[k].wait_recv()
        for j in range(per):
            total = w_keep[first.start + j, row, :]
            for k in range(1, n):
                total = total + rs_in[k, j]
            piece_buf[j] = tied3[first.start + j, row, :] * (0.5 * total) / piece_buf[j]
        for k in range(1, n):
            ag_copies[k].start()
            fw_copies[k].start()
        fw_copies[0].start()

    owner_only(me, own_piece)

    def arrived(k):
        def go():
            ag_copies[k].wait_recv()
        return go

    for k in range(1, n):
        owner_only(source(k), arrived(k))
    owner_only(me, fw_copies[0].wait)
    for k in range(1, n):
        owner_only(source(k), fw_copies[k].wait_recv)
    for k in range(1, n):
        owner_only(peer(k), rs_copies[k].wait_send)
        owner_only(me, ag_copies[k].wait_send)
        owner_only(me, fw_copies[k].wait_send)


def output_kernel(
    n, fresh, piece_buf, ag_in, fw_in, new_loadings, new_basis, nb, io_sem
):
    rank, pixels = nb.shape
    half, per, row_split = layout(n, rank, pixels)
    owners = half // per * row_split
    rows = rank // row_split
    me = lax.axis_index("scan")
    first_copy = pltpu.make_async_copy(fresh, new_loadings, io_sem.at[0])
    first_copy.start()

    def put(index, ref, flip):
        first, row = piece_at(index, per, row_split, rows)
        for j in range(per):
            block = first.start + j
            value = ref[j]
            if flip:
                block = pixels // LANES - 1 - block
                value = mirrored(value)
            nb[row, pl.ds(pl.multiple_of(block * LANES, LANES), LANES)] = value

    for k in range(n):
        index = lax.rem(me + n - k, n)

        def go():
            put(index, piece_buf if k == 0 else ag_in.at[k], False)
            put(index, fw_in.at[k], True)

        if owners == n:
            go()
        else:
            pl.when(index < owners)(go)
    second_copy = pltpu.make_async_copy(nb, new_basis, io_sem.at[1])
    second_copy.start()
    first_copy.wait()
    second_copy.wait()


def per_device(n, spectra, basis, loadings):
    rank, pixels = basis.shape
    positions = loadings.shape[1]
    blocks = pixels // LANES
    half, per, row_split = layout(n, rank, pixels)
    rows = rank // row_split
    load_chunks = 8
    pos_chunk = positions // 2
    col_chunk = 4 * LANES
    pack = LANES // rank
    dma = pltpu.SemaphoreType.DMA
    any_space = pl.BlockSpec(memory_space=pl.ANY)
    vmem = pl.BlockSpec(memory_space=pltpu.VMEM)
    hbm = pl.BlockSpec(memory_space=pltpu.HBM)
    inputs = [pltpu.with_memory_space_constraint(x, pltpu.HBM) for x in (spectra, basis, loadings)]
    parts = pl.pallas_call(
        functools.partial(tie_kernel, load_chunks, 4),
        out_shape=(
            pltpu.VMEM(spectra.shape, BF16),
            pltpu.VMEM(spectra.shape, BF16),
            pltpu.VMEM((blocks, rank, LANES), F32),
            pltpu.VMEM((2 * rank, pixels), BF16),
            pltpu.VMEM((rank, positions), F32),
            pltpu.VMEM((rank, positions), F32),
        ),
        in_specs=[hbm] * 3,
        out_specs=(vmem,) * 6,
        scratch_shapes=[
            pltpu.VMEM(spectra.shape, F32),
            pltpu.VMEM((rank, pixels), F32),
            pltpu.VMEM((rank, pixels), F32),
            dma((load_chunks,)),
            dma((2,)),
            dma((2,)),
        ],
        compiler_params=pltpu.CompilerParams(
            collective_id=0, has_side_effects=True, vmem_limit_bytes=32 << 20
        ),
        name="tie_and_split",
    )(*inputs)
    outs = pl.pallas_call(
        functools.partial(update_kernel, n, pos_chunk, col_chunk, 1),
        out_shape=(
            pltpu.VMEM(loadings.shape, F32),
            pltpu.VMEM((per, rows, LANES), F32),
            pltpu.VMEM((n, per, rows, LANES), F32),
            pltpu.VMEM((n, per, rows, LANES), F32),
        ),
        in_specs=[vmem] * 6,
        out_specs=(vmem,) * 4,
        scratch_shapes=[
            pltpu.VMEM((2 * rank, positions), BF16),
            pltpu.VMEM((positions // pos_chunk, rank, pos_chunk), F32),
            pltpu.VMEM((positions // pos_chunk, rank, pos_chunk), F32),
            pltpu.VMEM((half, rank, LANES), F32),
            pltpu.VMEM((half, rank, LANES), F32),
            pltpu.VMEM((half, rank, LANES), F32),
            pltpu.VMEM((n, per, rows, LANES), F32),
            pltpu.VMEM((rank // pack, LANES), F32),
            pltpu.VMEM((n, rank // pack, LANES), F32),
            dma((2, positions // pos_chunk)),
            dma((2, half * LANES // col_chunk)),
            dma((n,)), dma((n,)), dma((n,)), dma((n,)),
            dma((n,)), dma((n,)), dma((n,)), dma((n,)),
        ],
        compiler_params=pltpu.CompilerParams(
            collective_id=1, has_side_effects=True, vmem_limit_bytes=32 << 20
        ),
        name="update",
    )(*parts)
    return pl.pallas_call(
        functools.partial(output_kernel, n),
        out_shape=(
            jax.ShapeDtypeStruct(loadings.shape, F32),
            jax.ShapeDtypeStruct(basis.shape, F32),
        ),
        in_specs=[vmem] * 4,
        out_specs=(any_space,) * 2,
        scratch_shapes=[pltpu.VMEM((rank, pixels), F32), dma((2,))],
        compiler_params=pltpu.CompilerParams(vmem_limit_bytes=8 << 20),
        name="write_out",
    )(*outs)


def solution(mesh):
    in_specs = (P(("grp", "scan"), "det"), P("grp", "det"), P("grp", "scan"))
    out_specs = (P("grp", "scan"), P("grp", "det"))
    return jax.shard_map(
        functools.partial(per_device, mesh.shape["scan"]),
        mesh=mesh, in_specs=in_specs, out_specs=out_specs, check_vma=False,
    )
```

```python
import functools

import jax
import jax.numpy as jnp
from jax import lax
from jax.experimental import pallas as pl
from jax.experimental.pallas import tpu as pltpu
from jax.sharding import PartitionSpec as P

HIGHEST = lax.Precision.HIGHEST
MESH = pl.DeviceIdType.MESH
F32 = jnp.float32
BF16 = jnp.bfloat16
LANES = 128


def split(x):
    hi = x.astype(BF16)
    lo = (x - hi.astype(F32)).astype(BF16)
    return hi, lo


def dot_nt(a, b):
    return lax.dot_general(a, b, (((1,), (1,)), ((), ())), preferred_element_type=F32)


def dot_nn(a, b):
    return lax.dot_general(a, b, (((1,), (0,)), ((), ())), preferred_element_type=F32)


def mirrored(x):
    index = (LANES - 1) - lax.broadcasted_iota(jnp.int32, x.shape, 1)
    return jnp.take_along_axis(x, index, axis=1, mode="promise_in_bounds")


def remote(src, dst, send, recv, where):
    return pltpu.make_async_remote_copy(
        src_ref=src, dst_ref=dst, send_sem=send, recv_sem=recv,
        device_id=where, device_id_type=MESH,
    )


def layout(n, rank, pixels):
    half = pixels // LANES // 2
    if n <= half:
        per, row_split = half // n, 1
    else:
        per, row_split = 1, min(n // half, rank // 8)
    return half, per, row_split


def piece_at(index, per, row_split, rows):
    first = index // row_split * per
    row = pl.multiple_of(lax.rem(index, row_split) * rows, 8) if row_split > 1 else 0
    return pl.ds(first, per), pl.ds(row, rows)


def tie_kernel(
    load_chunks, early,
    spectra, basis, loadings,
    s_hi, s_lo, tied3, tied2, load, weighted,
    sbuf, own, other, sp_sem, io_sem, bs_sem,
):
    rank, pixels = basis.shape
    positions = loadings.shape[1]
    blocks = pixels // LANES
    partner = {"det": 1 - lax.axis_index("det")}
    barrier = pltpu.get_barrier_semaphore()
    pl.semaphore_signal(barrier, inc=1, device_id=partner, device_id_type=MESH)

    load_rows = positions // load_chunks
    spectra_copies = []
    for i in range(load_chunks):
        part = pl.ds(i * load_rows, load_rows)
        spectra_copies.append(
            pltpu.make_async_copy(spectra.at[part], sbuf.at[part], sp_sem.at[i])
        )
    own_copy = pltpu.make_async_copy(basis, own, io_sem.at[0])
    load_copy = pltpu.make_async_copy(loadings, load, io_sem.at[1])
    basis_copy = remote(basis, other, bs_sem.at[0], bs_sem.at[1], partner)
    for i in range(early):
        spectra_copies[i].start()
    pl.semaphore_wait(barrier, 1)
    basis_copy.start()
    own_copy.start()
    load_copy.start()
    for i in range(early, load_chunks):
        spectra_copies[i].start()

    def divide(i):
        spectra_copies[i].wait()

        @pl.loop(0, load_rows // 16, unroll=True)
        def _(j):
            part = pl.ds(pl.multiple_of(i * load_rows + j * 16, 16), 16)
            hi, lo = split(sbuf[part, :])
            s_hi[part, :] = hi
            s_lo[part, :] = lo

    for i in range(early):
        divide(i)
    own_copy.wait()
    basis_copy.wait()
    for b in range(blocks):
        mine = own[:, b * LANES:(b + 1) * LANES]
        back = blocks - 1 - b
        tied = 0.5 * (mine + mirrored(other[:, back * LANES:(back + 1) * LANES]))
        tied3[b] = tied
        hi, lo = split(tied)
        tied2[:rank, b * LANES:(b + 1) * LANES] = hi
        tied2[rank:, b * LANES:(b + 1) * LANES] = lo
    squares = dot_nt(tied2[...], tied2[...])
    gram = 2.0 * (
        squares[:rank, :rank] + (squares[:rank, rank:] + squares[rank:, :rank])
    )
    load_copy.wait()
    weighted[...] = jnp.dot(
        gram, load[...], precision=HIGHEST, preferred_element_type=F32
    )
    for i in range(early, load_chunks):
        divide(i)


def update_kernel(
    n, pos_chunk, col_chunk, wait_at,
    s_hi, s_lo, tied3, tied2, load, weighted,
    new_loadings, piece_buf, ag_in, fw_in,
    nl2, num_out, num_in, w_keep, w_out, w_in, rs_in, cr_out, cr_in,
    nm_sem, w_sem, rs_send, rs_recv, cr_send, cr_recv,
    ag_send, ag_recv, fw_send, fw_recv,
):
    blocks, rank, _ = tied3.shape
    half, per, row_split = layout(n, rank, blocks * LANES)
    owners = half // per * row_split
    rows = rank // row_split
    pack = LANES // rank
    me = lax.axis_index("scan")
    partner = {"det": 1 - lax.axis_index("det")}

    def peer(k):
        return lax.rem(me + k, n)

    def source(k):
        return lax.rem(me + n - k, n)

    def owner_only(index, fn):
        if owners == n:
            fn()
        else:
            pl.when(index < owners)(fn)

    barrier = pltpu.get_barrier_semaphore()
    for k in range(1, n):
        pl.semaphore_signal(barrier, inc=1, device_id={"scan": peer(k)}, device_id_type=MESH)
    pl.semaphore_signal(barrier, inc=1, device_id=partner, device_id_type=MESH)
    for k in range(1, n):
        pl.semaphore_signal(
            barrier, inc=1, device_id={"scan": peer(k), **partner}, device_id_type=MESH
        )
    positions = load.shape[1]
    chunks = positions // pos_chunk
    num_copies = [
        remote(num_out.at[i], num_in.at[i], nm_sem.at[0, i], nm_sem.at[1, i], partner)
        for i in range(chunks)
    ]

    def products(i):
        part = pl.ds(i * pos_chunk, pos_chunk)
        both = dot_nt(s_hi[part, :], tied2[...])
        low = dot_nt(s_lo[part, :], tied2[:rank, :])
        num_out[i] = (both[:, :rank] + (both[:, rank:] + low)).T

    def update(i):
        num_copies[i].wait()
        cols = slice(i * pos_chunk, (i + 1) * pos_chunk)
        fresh = load[:, cols] * (num_out[i] + num_in[i]) / weighted[:, cols]
        new_loadings[:, cols] = fresh
        hi, lo = split(fresh)
        nl2[:rank, cols] = hi
        nl2[rank:, cols] = lo

    for i in range(chunks):
        products(i)
        if i == wait_at:
            pl.semaphore_wait(barrier, 2 * n - 1)
            for j in range(i):
                num_copies[j].start()
        if i >= wait_at:
            num_copies[i].start()
    for i in range(chunks):
        update(i)

    def sums(cols):
        both = dot_nn(nl2[...], s_hi[:, cols])
        low = dot_nn(nl2[:rank, :], s_lo[:, cols])
        return both[:rank] + (both[rank:] + low)

    step = col_chunk // LANES
    count = half // step
    w_copies = []
    for i in range(count):
        part = pl.ds(i * step, step)
        w_copies.append(
            remote(w_out.at[part], w_in.at[part], w_sem.at[0, i], w_sem.at[1, i], partner)
        )
    cr_copies = [None]
    for k in range(1, n):
        cr_copies.append(
            remote(cr_out, cr_in.at[k], cr_send.at[k], cr_recv.at[k], {"scan": peer(k)})
        )
    for i in range(count):
        first = half + i * step
        value = sums(slice(first * LANES, (first + step) * LANES))
        for j in range(step):
            w_out[i * step + j] = value[:, j * LANES:(j + 1) * LANES]
        w_copies[i].start()
    squares = dot_nt(nl2[...], nl2[...])
    cross = squares[:rank, :rank] + (squares[:rank, rank:] + squares[rank:, :rank])
    cr_out[...] = jnp.concatenate(
        [cross[i * (rank // pack):(i + 1) * (rank // pack)] for i in range(pack)], axis=1
    )
    for k in range(1, n):
        cr_copies[k].start()

    for i in range(count):
        value = sums(slice(i * col_chunk, (i + 1) * col_chunk))
        for j in range(step):
            w_keep[i * step + j] = value[:, j * LANES:(j + 1) * LANES]
    for copy in w_copies:
        copy.wait()
    for b in range(half):
        w_keep[b] = w_keep[b] + mirrored(w_in[half - 1 - b])

    rs_copies = [None]
    for k in range(1, n):
        rs_copies.append(
            remote(
                w_keep.at[piece_at(peer(k), per, row_split, rows)], rs_in.at[k],
                rs_send.at[k], rs_recv.at[k], {"scan": peer(k)},
            )
        )
        owner_only(peer(k), rs_copies[k].start)

    for k in range(1, n):
        cr_copies[k].wait()
    total = cr_out[...]
    for k in range(1, n):
        total = total + cr_in[k]
    cross = jnp.concatenate(
        [total[:, i * rank:(i + 1) * rank] for i in range(pack)], axis=0
    )

    ag_copies = [None]
    for k in range(1, n):
        ag_copies.append(
            remote(piece_buf, ag_in.at[k], ag_send.at[k], ag_recv.at[k], {"scan": peer(k)})
        )
    fw_copies = [remote(piece_buf, fw_in.at[0], fw_send.at[0], fw_recv.at[0], partner)]
    for k in range(1, n):
        fw_copies.append(
            remote(
                piece_buf, fw_in.at[k], fw_send.at[k], fw_recv.at[k],
                {"scan": peer(k), **partner},
            )
        )

    def own_piece():
        first, row = piece_at(me, per, row_split, rows)
        for j in range(per):
            weights = jnp.dot(
                cross, tied3[first.start + j], precision=HIGHEST, preferred_element_type=F32
            )
            if row_split > 1:
                piece_buf[0] = weights[:rows]
                for i in range(1, row_split):
                    @pl.when(lax.rem(me, row_split) == i)
                    def _():
                        piece_buf[0] = weights[i * rows:(i + 1) * rows]
            else:
                piece_buf[j] = weights
        for k in range(1, n):
            rs_copies[k].wait_recv()
        for j in range(per):
            total = w_keep[first.start + j, row, :]
            for k in range(1, n):
                total = total + rs_in[k, j]
            piece_buf[j] = tied3[first.start + j, row, :] * (0.5 * total) / piece_buf[j]
        for k in range(1, n):
            ag_copies[k].start()
            fw_copies[k].start()
        fw_copies[0].start()

    owner_only(me, own_piece)

    def arrived(k):
        def go():
            ag_copies[k].wait_recv()
        return go

    for k in range(1, n):
        owner_only(source(k), arrived(k))
    owner_only(me, fw_copies[0].wait)
    for k in range(1, n):
        owner_only(source(k), fw_copies[k].wait_recv)
    for k in range(1, n):
        owner_only(peer(k), rs_copies[k].wait_send)
        owner_only(me, ag_copies[k].wait_send)
        owner_only(me, fw_copies[k].wait_send)


def output_kernel(
    n, fresh, piece_buf, ag_in, fw_in, new_loadings, new_basis, nb, io_sem
):
    rank, pixels = nb.shape
    half, per, row_split = layout(n, rank, pixels)
    owners = half // per * row_split
    rows = rank // row_split
    me = lax.axis_index("scan")
    first_copy = pltpu.make_async_copy(fresh, new_loadings, io_sem.at[0])
    first_copy.start()

    def put(index, ref, flip):
        first, row = piece_at(index, per, row_split, rows)
        for j in range(per):
            block = first.start + j
            value = ref[j]
            if flip:
                block = pixels // LANES - 1 - block
                value = mirrored(value)
            nb[row, pl.ds(pl.multiple_of(block * LANES, LANES), LANES)] = value

    for k in range(n):
        index = lax.rem(me + n - k, n)

        def go():
            put(index, piece_buf if k == 0 else ag_in.at[k], False)
            put(index, fw_in.at[k], True)

        if owners == n:
            go()
        else:
            pl.when(index < owners)(go)
    second_copy = pltpu.make_async_copy(nb, new_basis, io_sem.at[1])
    second_copy.start()
    first_copy.wait()
    second_copy.wait()


def per_device(n, spectra, basis, loadings):
    rank, pixels = basis.shape
    positions = loadings.shape[1]
    blocks = pixels // LANES
    half, per, row_split = layout(n, rank, pixels)
    rows = rank // row_split
    load_chunks = 8
    pos_chunk = positions // 2
    col_chunk = 8 * LANES
    pack = LANES // rank
    dma = pltpu.SemaphoreType.DMA
    any_space = pl.BlockSpec(memory_space=pl.ANY)
    vmem = pl.BlockSpec(memory_space=pltpu.VMEM)
    hbm = pl.BlockSpec(memory_space=pltpu.HBM)
    inputs = [pltpu.with_memory_space_constraint(x, pltpu.HBM) for x in (spectra, basis, loadings)]
    parts = pl.pallas_call(
        functools.partial(tie_kernel, load_chunks, 6),
        out_shape=(
            pltpu.VMEM(spectra.shape, BF16),
            pltpu.VMEM(spectra.shape, BF16),
            pltpu.VMEM((blocks, rank, LANES), F32),
            pltpu.VMEM((2 * rank, pixels), BF16),
            pltpu.VMEM((rank, positions), F32),
            pltpu.VMEM((rank, positions), F32),
        ),
        in_specs=[hbm] * 3,
        out_specs=(vmem,) * 6,
        scratch_shapes=[
            pltpu.VMEM(spectra.shape, F32),
            pltpu.VMEM((rank, pixels), F32),
            pltpu.VMEM((rank, pixels), F32),
            dma((load_chunks,)),
            dma((2,)),
            dma((2,)),
        ],
        compiler_params=pltpu.CompilerParams(
            collective_id=0, has_side_effects=True, vmem_limit_bytes=32 << 20
        ),
        name="tie_and_split",
    )(*inputs)
    outs = pl.pallas_call(
        functools.partial(update_kernel, n, pos_chunk, col_chunk, 1),
        out_shape=(
            pltpu.VMEM(loadings.shape, F32),
            pltpu.VMEM((per, rows, LANES), F32),
            pltpu.VMEM((n, per, rows, LANES), F32),
            pltpu.VMEM((n, per, rows, LANES), F32),
        ),
        in_specs=[vmem] * 6,
        out_specs=(vmem,) * 4,
        scratch_shapes=[
            pltpu.VMEM((2 * rank, positions), BF16),
            pltpu.VMEM((positions // pos_chunk, rank, pos_chunk), F32),
            pltpu.VMEM((positions // pos_chunk, rank, pos_chunk), F32),
            pltpu.VMEM((half, rank, LANES), F32),
            pltpu.VMEM((half, rank, LANES), F32),
            pltpu.VMEM((half, rank, LANES), F32),
            pltpu.VMEM((n, per, rows, LANES), F32),
            pltpu.VMEM((rank // pack, LANES), F32),
            pltpu.VMEM((n, rank // pack, LANES), F32),
            dma((2, positions // pos_chunk)),
            dma((2, half * LANES // col_chunk)),
            dma((n,)), dma((n,)), dma((n,)), dma((n,)),
            dma((n,)), dma((n,)), dma((n,)), dma((n,)),
        ],
        compiler_params=pltpu.CompilerParams(
            collective_id=1, has_side_effects=True, vmem_limit_bytes=32 << 20
        ),
        name="update",
    )(*parts)
    return pl.pallas_call(
        functools.partial(output_kernel, n),
        out_shape=(
            jax.ShapeDtypeStruct(loadings.shape, F32),
            jax.ShapeDtypeStruct(basis.shape, F32),
        ),
        in_specs=[vmem] * 4,
        out_specs=(any_space,) * 2,
        scratch_shapes=[pltpu.VMEM((rank, pixels), F32), dma((2,))],
        compiler_params=pltpu.CompilerParams(vmem_limit_bytes=8 << 20),
        name="write_out",
    )(*outs)


def solution(mesh):
    in_specs = (P(("grp", "scan"), "det"), P("grp", "det"), P("grp", "scan"))
    out_specs = (P("grp", "scan"), P("grp", "det"))
    return jax.shard_map(
        functools.partial(per_device, mesh.shape["scan"]),
        mesh=mesh, in_specs=in_specs, out_specs=out_specs, check_vma=False,
    )
```
